256 devices in a mesh: build: 16 (over x, y_hi, core), lat: 16 (over y_lo, z).
Axes of the slice: x: 4, y: 4 (y_hi: 2, y_lo: 2; y = y_hi * 2 + y_lo), z: 8, core: 2. Of those that a mesh axis runs over, the one named last changes fastest.
Arguments:
- density: float32 [32, 256, 1024], P('build', 'lat'), may hold values from 0.03 to 1
- support_mask: int32 [256, 1024], P('lat'), may hold values from 0 to 1
- pattern: int32 [27], replicated, may hold values from 0 to 7
- blocks: float32 [8, 3, 3], replicated, may hold values from -0.625 to 0.625
- displacement: float32 [3, 32, 256, 1024], P(None, 'build', 'lat'), may hold values from -6 to 6
- adjoint: float32 [3, 32, 256, 1024], P(None, 'build', 'lat'), may hold values from -6 to 6
Outputs:
- force: float32 [3, 32, 256, 1024], P(None, 'build', 'lat')
- sensitivity: float32 [32, 256, 1024], P('build', 'lat')
The draws below stay inside these ranges and needn't reach their ends.
All inputs are finite; a program needn't handle non-finite values.
Results may differ from the reference program's by a relative error of at most 0.0003.
Values sent between devices are 32-bit elements; how exact they have to be, the bound alone decides.
No kernel may reach another device: no remote copies, remote signals or barrier semaphores. Data moves between devices by JAX's collectives and lax.ppermute only.
A program may use at most 64 MiB of HBM per device.

```python
import jax
import jax.numpy as jnp
from jax import lax

CX = 16
NY = 1024
NB = 8
NZ = 32
NX = 256


def draw_density(key, part):
    phase_key = jax.random.fold_in(key, 101)
    lower_key = jax.random.fold_in(key, 202)
    upper_key = jax.random.fold_in(key, 303)
    phase = jax.random.randint(phase_key, (), 0, 2)
    layers = jnp.arange(NZ, dtype=jnp.int32)[:, None, None]
    rows = jnp.arange(NX, dtype=jnp.int32)[None, :, None]
    open_cells = ((layers + rows + phase) % 2 == 1).astype(jnp.float32)
    lower_draw = jax.random.uniform(lower_key, (NZ, NX, NY), jnp.float32)
    upper_draw = jax.random.uniform(upper_key, (NZ, NX, NY), jnp.float32)
    lower_values = 0.03 + 0.02 * lower_draw
    upper_values = 0.65 + 0.35 * upper_draw
    return open_cells * upper_values + (1.0 - open_cells) * lower_values


def draw_support_mask(key, part):
    period = CX * ((2 * NZ + 2 * CX - 3) // CX)
    rows = jnp.arange(NX, dtype=jnp.int32)
    rail = ((rows + NZ - 1) % period == 0) | (rows == NX - 1)
    coverage = jax.random.randint(jax.random.fold_in(key, 404), (NX, NY), 0, 4)
    return (rail[:, None] & (coverage > 0)).astype(jnp.int32)


def set_ends(values, stream_key, smallest, largest):
    dims = values.shape
    spot = [jax.random.randint(jax.random.fold_in(stream_key, axis), (), 0, dims[axis]) for axis in range(len(dims))]
    values = values.at[tuple(spot)].set(smallest)
    longest = dims.index(max(dims))
    spot[longest] = (spot[longest] + 1) % dims[longest]
    return values.at[tuple(spot)].set(largest)


def block_levels(rng, extent, split, smallest, high):
    def one(dim, parts):
        draws = jax.random.uniform(jax.random.fold_in(jax.random.fold_in(rng, 6), dim), (parts,), jnp.float32, smallest / len(split), high / len(split))
        return jnp.repeat(jnp.exp(draws), extent[dim] // parts).reshape((-1,) + (1,) * (len(extent) - dim - 1))

    gain = one(*split[0])
    for cut in split[1:]:
        gain = gain * one(*cut)
    return gain


def centred(key, dims, deviation, bound, pieces=(), kind=jnp.bfloat16):
    drawn = jax.random.normal(key, dims, jnp.float32) * deviation
    if len(pieces) > 0:
        drawn = block_levels(key, dims, pieces, -0.22, 0.18) * drawn
    return jnp.clip(drawn, min=-bound, max=bound).astype(kind)


def setup_inputs(seed: int = 0) -> dict:
    streams_of = jax.random.split(jax.random.key(seed), 7)
    density = draw_density(jax.random.fold_in(streams_of[6], 71), 0)
    support_mask = draw_support_mask(jax.random.fold_in(streams_of[6], 71), 0)
    pattern = set_ends(jax.random.randint(streams_of[2], (27,), 0, NB), jax.random.fold_in(streams_of[2], 1), 0, NB - 1).astype(jnp.int32)
    blocks = centred(streams_of[3], (NB, 3, 3), 81 ** -0.5, 0.625, (), jnp.float32)
    displacement = centred(streams_of[4], (3, NZ, NX, NY), 1.0, 6.0, ((1, 16), (2, 16)), jnp.float32)
    adjoint = centred(streams_of[5], (3, NZ, NX, NY), 1.0, 6.0, ((1, 16), (2, 16)), jnp.float32)
    return dict(density=density, support_mask=support_mask, pattern=pattern, blocks=blocks, displacement=displacement, adjoint=adjoint)


exponent = 16.0
smooth_eps = 0.0001
root_eps = 0.01
base_floor = 0.05
modulus_floor = 0.001
highest = lax.Precision.HIGHEST

def cross_sum(layer_plane):
    padded = jnp.pad(layer_plane, 1)
    centre = padded[1:-1, 1:-1]
    return centre + padded[:-2, 1:-1] + padded[2:, 1:-1] + padded[1:-1, :-2] + padded[1:-1, 2:]

def stencil(values_in, blocks_used, reverse):
    padded = jnp.pad(values_in, ((0, 0), (1, 1), (1, 1), (1, 1)))
    layer_count, width_x, width_y = values_in.shape[1:]
    result = jnp.zeros(values_in.shape, jnp.float32)
    direction = -1 if reverse else 1
    number = 0
    for step_z in (-1, 0, 1):
        for step_x in (-1, 0, 1):
            for step_y in (-1, 0, 1):
                start_z = 1 + direction * step_z
                start_x = 1 + direction * step_x
                start_y = 1 + direction * step_y
                shifted = padded[:, start_z:start_z + layer_count, start_x:start_x + width_x, start_y:start_y + width_y]
                matrix = blocks_used[number].T if reverse else blocks_used[number]
                result = result + jnp.einsum('cd,dzxy->czxy', matrix, shifted, precision=highest)
                number += 1
    return result

def reference(density, support_mask, pattern, blocks, displacement, adjoint):
    base_plane = base_floor + (1.0 - base_floor) * support_mask.astype(jnp.float32)

    def forward_layer(from_below, design_layer):
        support = cross_sum(from_below ** exponent) ** (1.0 / exponent)
        differ = design_layer - support
        printed = 0.5 * (design_layer + support - jnp.sqrt(differ * differ + smooth_eps) + root_eps)
        return (printed, (printed, support))
    _, (printed, support) = lax.scan(forward_layer, base_plane, density)
    modulus = modulus_floor + (1.0 - modulus_floor) * printed ** 3
    blocks_used = blocks[pattern]
    force = stencil(modulus[None] * displacement, blocks_used, False)
    pulled = stencil(adjoint, blocks_used, True)
    direct = lax.optimization_barrier(jnp.sum(displacement * pulled, axis=0)) * (3.0 * (1.0 - modulus_floor)) * printed ** 2

    def backward_layer(from_above, layer_items):
        direct_layer, printed_layer, support_layer, design_layer = layer_items
        weight_total = direct_layer + printed_layer ** (exponent - 1.0) * cross_sum(from_above)
        differ = design_layer - support_layer
        slope_term = differ / jnp.sqrt(differ * differ + smooth_eps)
        sensitivity = weight_total * 0.5 * (1.0 - slope_term)
        passed = weight_total * 0.5 * (1.0 + slope_term) / support_layer ** (exponent - 1.0)
        return (passed, sensitivity)
    zero_plane = jnp.zeros(density.shape[1:], jnp.float32)
    _, sensitivity = lax.scan(backward_layer, zero_plane, (direct, printed, support, density), reverse=True)
    return (force, sensitivity)
```

```python
import functools

import jax
import jax.numpy as jnp
from jax import lax
from jax.experimental import pallas as pl
from jax.experimental.pallas import tpu as pltpu
from jax.sharding import PartitionSpec as P

smooth_eps = 0.0001
root_eps = 0.01
base_floor = 0.05
modulus_floor = 0.001
f32 = jnp.float32
bf16 = jnp.bfloat16
VM = pl.BlockSpec(memory_space=pltpu.VMEM)
SM = pl.BlockSpec(memory_space=pltpu.SMEM)


def call(kernel, outs, args, scratch=(), smem=0, cost=2000000):
    specs = [SM] * smem + [VM] * (len(args) - smem)
    return pl.pallas_call(
        kernel,
        out_shape=[jax.ShapeDtypeStruct(s, d) for s, d in outs],
        in_specs=specs,
        out_specs=[VM] * len(outs),
        scratch_shapes=list(scratch),
        cost_estimate=pl.CostEstimate(flops=cost, bytes_accessed=cost, transcendentals=0),
    )(*args)


def lane(shape):
    return lax.broadcasted_iota(jnp.int32, shape, len(shape) - 1)


def row(shape):
    return lax.broadcasted_iota(jnp.int32, shape, len(shape) - 2)


def shifted_tiles(x):
    tiles = x.shape[1] // 128
    moved = pltpu.roll(x, 32, 1)
    cut = [moved[:, 128 * t : 128 * t + 128] for t in range(tiles)]
    low = lane(cut[0].shape) < 32
    zero = jnp.zeros_like(cut[0])
    return (
        [zero, jnp.where(low, zero, cut[0])]
        + cut[1:]
        + [jnp.where(low, cut[0], zero), zero]
    )


def prepare_density(dens_ref, out_ref):
    x = dens_ref[...].reshape(32, 1024)
    s = shifted_tiles(x)
    w = [pltpu.roll(t, 64, 1) for t in s]
    low = lane(s[0].shape) < 64
    for p in range(16):
        k = p // 2 + 1
        if p % 2 == 0:
            first, second = s[k], jnp.where(low, s[k + 1], s[k - 1])
        else:
            first, second = jnp.where(low, w[k], w[k + 1]), jnp.where(low, w[k + 1], w[k])
        out_ref[p, :, :, 0:128] = first.reshape(2, 16, 128)
        out_ref[p, :, :, 128:256] = second.reshape(2, 16, 128)


def prepare_fields(pq_ref, disp_ref, adj_ref, mask_ref, out_ref, base_ref, wide_ref):
    for number, ref in ((0, disp_ref), (3, adj_ref)):
        for c in range(3):
            s = shifted_tiles(ref[c].reshape(32, 1024))
            w = [pltpu.roll(t, 64, 1) for t in s]
            low = lane(s[0].shape) < 64
            for p in range(16):
                k = p // 2 + 1
                first = s[k] if p % 2 == 0 else jnp.where(low, w[k], w[k + 1])
                out_ref[p, number + c] = first.reshape(2, 16, 128)
    base = base_floor + (1.0 - base_floor) * mask_ref[...].astype(f32)
    for t, tile in enumerate(shifted_tiles(base)):
        wide_ref[:, 128 * t : 128 * t + 128] = tile
    p = pq_ref[0]
    k = lax.div(p, 2)
    odd = (p - 2 * k).astype(f32)
    before, here, after = [wide_ref[:, pl.ds(pl.multiple_of((k + t) * 128, 128), 128)] for t in range(3)]
    here2, after2 = pltpu.roll(here, 64, 1), pltpu.roll(after, 64, 1)
    low = lane(here.shape) < 64
    even0, even1 = here, jnp.where(low, after, before)
    odd0, odd1 = jnp.where(low, here2, after2), jnp.where(low, after2, here2)
    base_ref[:, 0:128] = even0 * (1.0 - odd) + odd0 * odd
    base_ref[:, 128:256] = even1 * (1.0 - odd) + odd1 * odd


def matrices(pattern_ref, blocks_ref, out_ref):
    k = lane((8, 256))
    dk = jnp.where(k < 192, k >> 6, (k - 192) >> 3)
    zk = jnp.where(k < 192, (k >> 4) & 3, ((k - 192) >> 1) & 3)
    at = [[(dk == d) & (zk == z) for z in range(4)] for d in range(3)]
    k2 = lane((16, 256))
    xk = jnp.where(k2 < 192, k2 & 15, jnp.where((k2 & 1) == 0, -1, 16))
    step = xk - row((16, 256))
    for kind in range(2):
        for ds in (-1, 0, 1):
            for c in range(3):
                rows = [[None] * 3, [None] * 3]
                for db in (-1, 0, 1):
                    values = {}
                    for da in (-1, 0, 1):
                        sign = -1 if kind == 0 else 1
                        o = 9 * (sign * da + 1) + 3 * (sign * db + 1) + (sign * ds + 1)
                        start = pattern_ref[o] * 9
                        for d in range(3):
                            values[da, d] = blocks_ref[start + (d * 3 + c if kind == 0 else c * 3 + d)]
                    for zi in range(2):
                        r = jnp.zeros((8, 256), f32)
                        for da in (-1, 0, 1):
                            for d in range(3):
                                r = jnp.where(at[d][da + 1 + zi], values[da, d], r)
                        rows[zi][db + 1] = r
                for zi in range(2):
                    m = jnp.zeros((16, 256), f32)
                    for db in (-1, 0, 1):
                        r = rows[zi][db + 1]
                        m = jnp.where(step == db, jnp.concatenate([r, r], 0), m)
                    high = m.astype(bf16)
                    low = (m - high.astype(f32)).astype(bf16)
                    start = ((ds + 1) * 6 + c * 2 + zi) * 16
                    out_ref[2 * kind, start : start + 16] = high
                    out_ref[2 * kind + 1, start : start + 16] = low


def pack_density(dens_ref, base_ref, up_ref, down_ref):
    up_ref[0:16] = base_ref[...]
    down_ref[0:16] = base_ref[...]
    for ph in range(2):
        for j in range(15):
            x = dens_ref[16 * ph + j]
            if j < 7:
                start = 16 + ph * 176 + j * 16
                up_ref[start : start + 16] = x
                down_ref[start : start + 16] = x
            else:
                start = 16 + ph * 176 + 112 + (j - 7) * 8
                up_ref[start : start + 8] = x[0:8]
                down_ref[start : start + 8] = x[8:16]


def cross_of(x):
    rows, width = x.shape
    return (
        x
        + pltpu.roll(x, 1, 0)
        + pltpu.roll(x, rows - 1, 0)
        + pltpu.roll(x, 1, 1)
        + pltpu.roll(x, width - 1, 1)
    )


def forward(ph, pq_ref, dens_ref, upper_ref, lower_ref, own_ref, *refs):
    if ph == 0:
        up, down = upper_ref[0:16], lower_ref[0:16]
        printed_ref, support_ref, state_ref = refs
    else:
        su_ref, sd_ref, printed_ref, support_ref, state_ref = refs
        up, down = su_ref[...], sd_ref[...]
    p, q = pq_ref[0], pq_ref[1]
    current = jnp.concatenate([up, own_ref[...], down], 0)
    l = lane((48, 256))
    y = 64 * p - 32 + l - jnp.where(l < 192, 0, 256)
    x = 16 * q - 16 + row((48, 256))
    inside = jnp.where((x >= 0) & (x < 256) & (y >= 0) & (y < 1024), 1.0, 0.0)
    rows = 48
    for j in range(16):
        p2 = current * current
        p4 = p2 * p2
        p8 = p4 * p4
        edge = (48 - rows) // 2
        cross = cross_of(p8 * p8 * inside[edge : 48 - edge])
        count = 48 if j < 7 else (32 if j < 15 else 16)
        if count < rows:
            cross = cross[8 : rows - 8]
        rows = count
        design = dens_ref[16 * ph + j]
        if j < 15:
            size = 16 if j < 7 else 8
            start = 16 + ph * 176 + (j * 16 if j < 7 else 112 + (j - 7) * 8)
            design = jnp.concatenate(
                [upper_ref[start : start + size], design, lower_ref[start : start + size]], 0
            )
        support = jnp.sqrt(jnp.sqrt(jnp.sqrt(jnp.sqrt(cross))))
        differ = design - support
        current = 0.5 * (design + support - jnp.sqrt(differ * differ + smooth_eps) + root_eps)
        edge = (rows - 16) // 2
        printed_ref[j] = current[edge : edge + 16, 0:128]
        support_ref[j] = support[edge : edge + 16, 0:128]
    state_ref[...] = current


def pack_rows(fields_ref, up_ref, down_ref):
    for c in range(3):
        for z in range(32):
            x = fields_ref[z // 2, 3 + c, z % 2]
            up_ref[c * 32 + z : c * 32 + z + 1] = x[0:1]
            down_ref[c * 32 + z : c * 32 + z + 1] = x[15:16]


def fill_halo(halo, upper, lower):
    halo[...] = jnp.zeros(halo.shape, f32)
    for c in range(3):
        halo[c, pl.ds(2, 32, stride=2)] = upper[c * 32 : c * 32 + 32]
        halo[c, pl.ds(3, 32, stride=2)] = lower[c * 32 : c * 32 + 32]


def product(field, halo, mat_ref, kind, i):
    edges = [halo[d, pl.ds(pl.multiple_of(8 * i, 8), 16)] for d in range(3)]
    sides = []
    for pair in range(2):
        main = [field[d, pl.ds(4 * i + 2 * pair, 4)].reshape(64, 128) for d in range(3)]
        rim = [e[4 * pair : 4 * pair + 8] for e in edges]
        sides.append(jnp.concatenate(main + rim + [jnp.zeros((40, 128), f32)], 0))
    u = jnp.concatenate(sides, 1)
    high = u.astype(bf16)
    low = (u - high.astype(f32)).astype(bf16)
    dot = functools.partial(jnp.dot, preferred_element_type=f32)
    mat_high, mat_low = mat_ref[2 * kind], mat_ref[2 * kind + 1]
    out = dot(mat_high, high) + dot(mat_high, low) + dot(mat_low, high)

    def pick(pair, c, zi):
        parts = [
            out[(s * 6 + c * 2 + zi) * 16 : (s * 6 + c * 2 + zi) * 16 + 16, 128 * pair : 128 * pair + 128]
            for s in range(3)
        ]
        return parts[1] + pltpu.roll(parts[0], 1, 1) + pltpu.roll(parts[2], 127, 1)

    return pick


def edges_of(pq_ref):
    q = pq_ref[1]
    return jnp.where(q > 0, 1.0, 0.0), jnp.where(q < 15, 1.0, 0.0)


def direct_part(pq_ref, fields_ref, upper_ref, lower_ref, mat_ref, out_ref, field, halo):
    keep_up, keep_down = edges_of(pq_ref)
    fill_halo(halo, upper_ref[...] * keep_up, lower_ref[...] * keep_down)
    for c in range(3):
        field[c, 0] = jnp.zeros((16, 128), f32)
        field[c, 33] = jnp.zeros((16, 128), f32)
        for z in range(32):
            field[c, z + 1] = fields_ref[z // 2, 3 + c, z % 2]

    def body(i, carry):
        pick = product(field, halo, mat_ref, 0, i)
        for pair in range(2):
            for zi in range(2):
                total = fields_ref[2 * i + pair, 0, zi] * pick(pair, 0, zi)
                for c in (1, 2):
                    total = total + fields_ref[2 * i + pair, c, zi] * pick(pair, c, zi)
                out_ref[4 * i + 2 * pair + zi] = total
        return carry

    lax.fori_loop(0, 8, body, 0)


def coefficients(pq_ref, p0_ref, s0_ref, p1_ref, s1_ref, dens_ref, d0_ref, fields_ref, *refs):
    a_ref, b_ref, e_ref, f_ref, up_ref, down_ref = refs
    y = 64 * pq_ref[0] - 32 + lane((16, 128))
    inside = (y >= 0) & (y < 1024)
    for z in range(32):
        ph, j = divmod(z, 16)
        printed = (p0_ref, p1_ref)[ph][j]
        support = (s0_ref, s1_ref)[ph][j]
        design = dens_ref[z, :, 0:128]
        p2 = printed * printed
        p3 = p2 * printed
        modulus = modulus_floor + (1.0 - modulus_floor) * p3
        p6 = p3 * p3
        p15 = p6 * p6 * p3
        s2 = support * support
        s3 = s2 * support
        s6 = s3 * s3
        s15 = s6 * s6 * s3
        differ = design - support
        slope = differ / jnp.sqrt(differ * differ + smooth_eps)
        direct = d0_ref[z] * (3.0 * (1.0 - modulus_floor)) * p2
        gain = 0.5 * (1.0 + slope) / s15
        kept = 0.5 * (1.0 - slope)
        zero = jnp.zeros_like(direct)
        a = jnp.where(inside, direct * gain, zero)
        b = jnp.where(inside, p15 * gain, zero)
        a_ref[z] = a
        b_ref[z] = b
        e_ref[z] = direct * kept
        f_ref[z] = p15 * kept
        for number, value in ((0, a), (1, b)):
            start = (number * 2 + ph) * 176
            if 1 <= j <= 8:
                start += (j - 1) * 8
                up_ref[start : start + 8] = value[0:8]
                down_ref[start : start + 8] = value[8:16]
            elif j >= 9:
                start += 64 + (j - 9) * 16
                up_ref[start : start + 16] = value
                down_ref[start : start + 16] = value
        for c in range(3):
            u = modulus * fields_ref[z // 2, c, z % 2]
            start = 704 + c * 32 + z
            up_ref[start : start + 1] = u[0:1]
            down_ref[start : start + 1] = u[15:16]


def force_part(pq_ref, p0_ref, p1_ref, fields_ref, upper_ref, lower_ref, mat_ref, out_ref, field, halo):
    keep_up, keep_down = edges_of(pq_ref)
    fill_halo(halo, upper_ref[704:800] * keep_up, lower_ref[704:800] * keep_down)
    for c in range(3):
        field[c, 0] = jnp.zeros((16, 128), f32)
        field[c, 33] = jnp.zeros((16, 128), f32)
    for z in range(32):
        printed = (p0_ref, p1_ref)[z // 16][z % 16]
        modulus = modulus_floor + (1.0 - modulus_floor) * (printed * printed * printed)
        for c in range(3):
            field[c, z + 1] = modulus * fields_ref[z // 2, c, z % 2]

    def body(i, carry):
        pick = product(field, halo, mat_ref, 1, i)
        low = lane((16, 128)) < 64
        for pair in range(2):
            for c in range(3):
                first = pltpu.roll(pick(pair, c, 0), 96, 1)
                second = pltpu.roll(pick(pair, c, 1), 32, 1)
                out_ref[2 * i + pair, c] = jnp.where(low, first, second)
        return carry

    lax.fori_loop(0, 8, body, 0)


def backward(ph, pq_ref, a_ref, b_ref, e_ref, f_ref, upper_ref, lower_ref, *refs):
    keep_up, keep_down = edges_of(pq_ref)
    if ph == 1:
        sens_ref, state_ref = refs
        current = None
    else:
        own_ref, su_ref, sd_ref, sens1_ref, force_ref, out_ref = refs
        current = jnp.concatenate([su_ref[...] * keep_up, own_ref[...], sd_ref[...] * keep_down], 0)
    rows = 48
    low = lane((16, 128)) < 64
    later = None
    for j in range(15, -1, -1):
        z = 16 * ph + j
        count = 48 if j >= 9 else (32 if j >= 1 else 16)
        sens = e_ref[z]
        coef = []
        for number, ref in ((0, a_ref), (1, b_ref)):
            value = ref[z]
            if j >= 1:
                size = 8 if j <= 8 else 16
                start = (number * 2 + ph) * 176 + ((j - 1) * 8 if j <= 8 else 64 + (j - 9) * 16)
                value = jnp.concatenate(
                    [
                        upper_ref[start : start + size] * keep_up,
                        value,
                        lower_ref[start : start + size] * keep_down,
                    ],
                    0,
                )
            coef.append(value)
        if current is None:
            current = coef[0]
        else:
            cross = cross_of(current)
            edge = (rows - 16) // 2
            sens = sens + f_ref[z] * cross[edge : edge + 16]
            if count < rows:
                cross = cross[8 : rows - 8]
            current = coef[0] + coef[1] * cross
        rows = count
        if j % 2 == 1:
            later = pltpu.roll(sens, 32, 1)
        else:
            packed = jnp.where(low, pltpu.roll(sens, 96, 1), later)
            if ph == 1:
                sens_ref[j // 2] = packed
            else:
                out_ref[j // 2, 3] = packed
    if ph == 1:
        state_ref[...] = current
    else:
        out_ref[:, 0:3] = force_ref[...]
        for i in range(8):
            out_ref[8 + i, 3] = sens1_ref[i]


def unpack(in_ref, force_ref, sens_ref):
    low = lane((16, 128)) < 64
    for k in range(8):
        for c in range(4):
            first, second = in_ref[2 * k, c], in_ref[2 * k + 1, c]
            layers = (
                jnp.where(low, first, pltpu.roll(second, 64, 1)),
                jnp.where(low, pltpu.roll(first, 64, 1), second),
            )
            for i in range(2):
                if c < 3:
                    force_ref[c, i, :, 128 * k : 128 * k + 128] = layers[i]
                else:
                    sens_ref[i, :, 128 * k : 128 * k + 128] = layers[i]


def trade(to_lower, to_upper):
    count = lax.axis_size("lat")
    up = [(i, (i + 1) % count) for i in range(count)]
    down = [(j, i) for i, j in up]
    return lax.ppermute(to_lower, "lat", up), lax.ppermute(to_upper, "lat", down)


def exchange(x):
    return lax.all_to_all(x, "build", 0, 0, tiled=True)


def on_device(density, support_mask, pattern, blocks, displacement, adjoint):
    pq = jnp.stack([lax.axis_index("build"), lax.axis_index("lat")]).astype(jnp.int32)
    (windows,) = call(prepare_density, [((16, 2, 16, 256), f32)], [density])
    dens = exchange(windows).reshape(32, 16, 256)
    fields, base = call(
        prepare_fields,
        [((16, 6, 2, 16, 128), f32), ((16, 256), f32)],
        [pq, displacement, adjoint, support_mask],
        scratch=[pltpu.VMEM((16, 11 * 128), f32)],
        smem=1,
    )
    (mats,) = call(matrices, [((4, 288, 256), bf16)], [pattern, blocks.reshape(72)], smem=2)
    fields = exchange(fields)
    up_send, down_send = call(pack_density, [((368, 256), f32)] * 2, [dens, base])
    upper, lower = trade(down_send, up_send)
    layer = ((16, 16, 128), f32)
    p0, s0, state = call(
        functools.partial(forward, 0),
        [layer, layer, ((16, 256), f32)],
        [pq, dens, upper, lower, base],
        smem=1,
    )
    state_up, state_down = trade(state, state)
    p1, s1, _ = call(
        functools.partial(forward, 1),
        [layer, layer, ((16, 256), f32)],
        [pq, dens, upper, lower, state, state_up, state_down],
        smem=1,
    )
    up_send, down_send = call(pack_rows, [((96, 128), f32)] * 2, [fields])
    adj_up, adj_down = trade(down_send, up_send)
    work = [pltpu.VMEM((3, 34, 16, 128), f32), pltpu.VMEM((3, 72, 128), f32)]
    (d0,) = call(
        direct_part,
        [((32, 16, 128), f32)],
        [pq, fields, adj_up, adj_down, mats],
        scratch=work,
        smem=1,
    )
    whole = ((32, 16, 128), f32)
    a, b, e, f, up_send, down_send = call(
        coefficients,
        [whole] * 4 + [((800, 128), f32)] * 2,
        [pq, p0, s0, p1, s1, dens, d0, fields],
        smem=1,
    )
    upper, lower = trade(down_send, up_send)
    sens1, state = call(
        functools.partial(backward, 1),
        [((8, 16, 128), f32), ((16, 128), f32)],
        [pq, a, b, e, f, upper, lower],
        smem=1,
    )
    state_up, state_down = trade(state, state)
    (force,) = call(
        force_part,
        [((16, 3, 16, 128), f32)],
        [pq, p0, p1, fields, upper, lower, mats],
        scratch=work,
        smem=1,
    )
    (packed,) = call(
        functools.partial(backward, 0),
        [((16, 4, 16, 128), f32)],
        [pq, a, b, e, f, upper, lower, state, state_up, state_down, sens1, force],
        smem=1,
    )
    packed = exchange(packed)
    return tuple(call(unpack, [((3, 2, 16, 1024), f32), ((2, 16, 1024), f32)], [packed]))


def solution(mesh):
    in_specs = (
        P("build", "lat", None),
        P("lat", None),
        P(),
        P(),
        P(None, "build", "lat", None),
        P(None, "build", "lat", None),
    )
    out_specs = (P(None, "build", "lat", None), P("build", "lat", None))
    return jax.shard_map(
        on_device, mesh=mesh, in_specs=in_specs, out_specs=out_specs, check_vma=False
    )
```

```python
import functools

import jax
import jax.numpy as jnp
from jax import lax
from jax.experimental import pallas as pl
from jax.experimental.pallas import tpu as pltpu
from jax.sharding import PartitionSpec as P


smooth_eps = 0.0001
root_eps = 0.01
base_floor = 0.05
modulus_floor = 0.001
f32 = jnp.float32
bf16 = jnp.bfloat16
VM = pl.BlockSpec(memory_space=pltpu.VMEM)
SM = pl.BlockSpec(memory_space=pltpu.SMEM)


def call(kernel, outs, args, scratch=(), smem=0, micros=1.0, room=6):
    specs = [SM] * smem + [VM] * (len(args) - smem)
    name = getattr(kernel, "func", kernel).__name__
    if isinstance(kernel, functools.partial):
        name += str(kernel.args[0])
    return run(kernel, outs, args, specs, scratch, micros, room)


def run(kernel, outs, args, specs, scratch, micros, room):
    return pl.pallas_call(
        kernel,
        out_shape=[jax.ShapeDtypeStruct(s, d) for s, d in outs],
        in_specs=specs,
        out_specs=[VM] * len(outs),
        scratch_shapes=list(scratch),
        compiler_params=pltpu.CompilerParams(vmem_limit_bytes=room << 20),
        cost_estimate=pl.CostEstimate(
            flops=0, bytes_accessed=int(micros * 3690000), transcendentals=0
        ),
    )(*args)


def lane(shape):
    return lax.broadcasted_iota(jnp.int32, shape, len(shape) - 1)


def row(shape):
    return lax.broadcasted_iota(jnp.int32, shape, len(shape) - 2)


def shifted_tiles(x):
    tiles = x.shape[1] // 128
    moved = pltpu.roll(x, 32, 1)
    cut = [moved[:, 128 * t : 128 * t + 128] for t in range(tiles)]
    low = lane(cut[0].shape) < 32
    zero = jnp.zeros_like(cut[0])
    return (
        [zero, jnp.where(low, zero, cut[0])]
        + cut[1:]
        + [jnp.where(low, cut[0], zero), zero]
    )


def prepare_density(dens_ref, out_ref):
    x = dens_ref[...].reshape(32, 1024)
    s = shifted_tiles(x)
    w = [pltpu.roll(t, 64, 1) for t in s]
    low = lane(s[0].shape) < 64
    for p in range(16):
        k = p // 2 + 1
        if p % 2 == 0:
            first, second = s[k], jnp.where(low, s[k + 1], s[k - 1])
        else:
            first, second = jnp.where(low, w[k], w[k + 1]), jnp.where(low, w[k + 1], w[k])
        out_ref[p, :, :, 0:128] = first.reshape(2, 16, 128)
        out_ref[p, :, :, 128:256] = second.reshape(2, 16, 128)


def pack_edges(disp_ref, adj_ref, up_ref, down_ref):
    for number, ref in ((0, disp_ref), (3, adj_ref)):
        for c in range(3):
            for i in range(2):
                start = (number + c) * 2 + i
                up_ref[start : start + 1] = ref[c, i, 0:1]
                down_ref[start : start + 1] = ref[c, i, 15:16]


def prepare_fields(disp_ref, adj_ref, mask_ref, upper_ref, lower_ref, out_ref, base_ref, wide_ref):
    def tiles_of(x):
        s = shifted_tiles(x)
        w = [pltpu.roll(t, 64, 1) for t in s]
        low = lane(s[0].shape) < 64
        for p in range(16):
            k = p // 2 + 1
            yield p, s[k] if p % 2 == 0 else jnp.where(low, w[k], w[k + 1])

    for number, ref in ((0, disp_ref), (3, adj_ref)):
        for c in range(3):
            start = (number + c) * 32
            for p, tile in tiles_of(ref[c].reshape(32, 1024)):
                out_ref[p, start : start + 32] = tile
    for h, (ref, keep) in enumerate(zip((upper_ref, lower_ref), edges_of())):
        for p, tile in tiles_of(ref[...] * keep):
            out_ref[p, pl.ds(192 + h, 12, stride=2)] = tile[0:12]
    base = base_floor + (1.0 - base_floor) * mask_ref[...].astype(f32)
    for t, tile in enumerate(shifted_tiles(base)):
        wide_ref[:, 128 * t : 128 * t + 128] = tile
    p = lax.axis_index("build")
    k = lax.div(p, 2)
    odd = (p - 2 * k).astype(f32)
    before, here, after = [wide_ref[:, pl.ds(pl.multiple_of((k + t) * 128, 128), 128)] for t in range(3)]
    here2, after2 = pltpu.roll(here, 64, 1), pltpu.roll(after, 64, 1)
    low = lane(here.shape) < 64
    even0, even1 = here, jnp.where(low, after, before)
    odd0, odd1 = jnp.where(low, here2, after2), jnp.where(low, after2, here2)
    base_ref[:, 0:128] = even0 * (1.0 - odd) + odd0 * odd
    base_ref[:, 128:256] = even1 * (1.0 - odd) + odd1 * odd


def matrices(pattern_ref, blocks_ref, out_ref):
    k = lane((8, 256))
    dk = jnp.where(k < 192, k >> 6, (k - 192) >> 3)
    zk = jnp.where(k < 192, (k >> 4) & 3, ((k - 192) >> 1) & 3)
    at = [[(dk == d) & (zk == z) for z in range(4)] for d in range(3)]
    k2 = lane((16, 256))
    xk = jnp.where(k2 < 192, k2 & 15, jnp.where((k2 & 1) == 0, -1, 16))
    step = xk - row((16, 256))
    for kind in range(2):
        for ds in (-1, 0, 1):
            for c in range(3):
                rows = [[None] * 3, [None] * 3]
                for db in (-1, 0, 1):
                    values = {}
                    for da in (-1, 0, 1):
                        sign = -1 if kind == 0 else 1
                        o = 9 * (sign * da + 1) + 3 * (sign * db + 1) + (sign * ds + 1)
                        start = pattern_ref[o]
                        for d in range(3):
                            values[da, d] = (
                                blocks_ref[start, d, c] if kind == 0 else blocks_ref[start, c, d]
                            )
                    for zi in range(2):
                        r = jnp.zeros((8, 256), f32)
                        for da in (-1, 0, 1):
                            for d in range(3):
                                r = jnp.where(at[d][da + 1 + zi], values[da, d], r)
                        rows[zi][db + 1] = r
                for zi in range(2):
                    m = jnp.zeros((16, 256), f32)
                    for db in (-1, 0, 1):
                        r = rows[zi][db + 1]
                        m = jnp.where(step == db, jnp.concatenate([r, r], 0), m)
                    high = m.astype(bf16)
                    low = (m - high.astype(f32)).astype(bf16)
                    start = ((ds + 1) * 6 + c * 2 + zi) * 16
                    out_ref[2 * kind, start : start + 16] = high
                    out_ref[2 * kind + 1, start : start + 16] = low


def pack_density(dens_ref, base_ref, up0_ref, down0_ref, up1_ref, down1_ref):
    up0_ref[176:192] = base_ref[...]
    down0_ref[176:192] = base_ref[...]
    for ph, up_ref, down_ref in ((0, up0_ref, down0_ref), (1, up1_ref, down1_ref)):
        for j in range(15):
            x = dens_ref[16 * ph + j]
            if j < 7:
                start = j * 16
                up_ref[start : start + 16] = x
                down_ref[start : start + 16] = x
            else:
                start = 112 + (j - 7) * 8
                up_ref[start : start + 8] = x[0:8]
                down_ref[start : start + 8] = x[8:16]


def cross_of(x):
    rows, width = x.shape
    return (
        x
        + pltpu.roll(x, 1, 0)
        + pltpu.roll(x, rows - 1, 0)
        + pltpu.roll(x, 1, 1)
        + pltpu.roll(x, width - 1, 1)
    )


def forward(ph, dens_ref, upper_ref, lower_ref, own_ref, *refs):
    if ph == 0:
        up, down = upper_ref[176:192], lower_ref[176:192]
        printed_ref, gain_ref, kept_ref, state_ref = refs
    else:
        su_ref, sd_ref, printed_ref, gain_ref, kept_ref, state_ref = refs
        up, down = su_ref[...], sd_ref[...]
    p, q = lax.axis_index("build"), lax.axis_index("lat")
    current = jnp.concatenate([up, own_ref[...], down], 0)
    l = lane((48, 256))
    y = 64 * p - 32 + l - jnp.where(l < 192, 0, 256)
    x = 16 * q - 16 + row((48, 256))
    inside = jnp.where((x >= 0) & (x < 256) & (y >= 0) & (y < 1024), 1.0, 0.0)
    rows = 48
    for j in range(16):
        p2 = current * current
        p4 = p2 * p2
        p8 = p4 * p4
        edge = (48 - rows) // 2
        cross = cross_of(p8 * p8 * inside[edge : 48 - edge])
        count = 48 if j < 7 else (32 if j < 15 else 16)
        if count < rows:
            cross = cross[8 : rows - 8]
        rows = count
        design = dens_ref[16 * ph + j]
        if j < 15:
            size = 16 if j < 7 else 8
            start = j * 16 if j < 7 else 112 + (j - 7) * 8
            design = jnp.concatenate(
                [upper_ref[start : start + size], design, lower_ref[start : start + size]], 0
            )
        support = lax.rsqrt(lax.rsqrt(lax.rsqrt(lax.rsqrt(cross))))
        differ = design - support
        square = differ * differ + smooth_eps
        inverse = lax.rsqrt(square)
        current = 0.5 * (design + support - square * inverse + root_eps)
        edge = (rows - 16) // 2
        printed_ref[j] = current[edge : edge + 16, 0:128]
        slope = (differ * inverse)[edge : edge + 16, 0:128]
        s1 = support[edge : edge + 16, 0:128]
        s3 = s1 * s1 * s1
        s6 = s3 * s3
        gain_ref[j] = 0.5 * (1.0 + slope) / (s6 * s6 * s3)
        kept_ref[j] = 0.5 * (1.0 - slope)
    state_ref[...] = current


def layer_of(fields_ref, c, z):
    start = (c * 2 + z % 2) * 16
    return fields_ref[z // 2, start : start + 16]


def product(field, halo, mat_ref, kind, i):
    edges = [halo[d, pl.ds(pl.multiple_of(8 * i, 8), 16)] for d in range(3)]
    sides = []
    for pair in range(2):
        main = [field[d, pl.ds(4 * i + 2 * pair, 4)].reshape(64, 128) for d in range(3)]
        rim = [e[4 * pair : 4 * pair + 8] for e in edges]
        sides.append(jnp.concatenate(main + rim + [jnp.zeros((40, 128), f32)], 0))
    u = jnp.concatenate(sides, 1)
    high = u.astype(bf16)
    low = (u - high.astype(f32)).astype(bf16)
    dot = functools.partial(jnp.dot, preferred_element_type=f32)
    mat_high, mat_low = mat_ref[2 * kind], mat_ref[2 * kind + 1]
    out = dot(mat_high, high) + dot(mat_high, low) + dot(mat_low, high)

    def pick(pair, c, zi):
        parts = [
            out[(s * 6 + c * 2 + zi) * 16 : (s * 6 + c * 2 + zi) * 16 + 16, 128 * pair : 128 * pair + 128]
            for s in range(3)
        ]
        return parts[1] + pltpu.roll(parts[0], 1, 1) + pltpu.roll(parts[2], 127, 1)

    return pick


def edges_of():
    q = lax.axis_index("lat")
    return jnp.where(q > 0, 1.0, 0.0), jnp.where(q < 15, 1.0, 0.0)


def direct_part(fields_ref, mat_ref, out_ref, field, halo):
    halo[...] = jnp.zeros(halo.shape, f32)
    for c in range(3):
        field[c, 0] = jnp.zeros((16, 128), f32)
        field[c, 33] = jnp.zeros((16, 128), f32)
        for z in range(32):
            field[c, z + 1] = layer_of(fields_ref, 3 + c, z)
        for k in range(16):
            start = 192 + (3 + c) * 4
            halo[c, 4 * k + 2 : 4 * k + 6] = fields_ref[k, start : start + 4]

    def body(i, carry):
        pick = product(field, halo, mat_ref, 0, i)
        for pair in range(2):
            for zi in range(2):
                total = fields_ref[2 * i + pair, zi * 16 : zi * 16 + 16] * pick(pair, 0, zi)
                for c in (1, 2):
                    start = (c * 2 + zi) * 16
                    total = total + fields_ref[2 * i + pair, start : start + 16] * pick(pair, c, zi)
                out_ref[4 * i + 2 * pair + zi] = total
        return carry

    lax.fori_loop(0, 8, body, 0)


def coefficients(p0_ref, g0_ref, k0_ref, p1_ref, g1_ref, k1_ref, d0_ref, *refs):
    a_ref, b_ref, e_ref, f_ref = refs[:4]
    y = 64 * lax.axis_index("build") - 32 + lane((16, 128))
    inside = (y >= 0) & (y < 1024)
    for z in range(32):
        ph, j = divmod(z, 16)
        printed = (p0_ref, p1_ref)[ph][j]
        gain = (g0_ref, g1_ref)[ph][j]
        kept = (k0_ref, k1_ref)[ph][j]
        p2 = printed * printed
        p3 = p2 * printed
        p6 = p3 * p3
        p15 = p6 * p6 * p3
        direct = d0_ref[z] * (3.0 * (1.0 - modulus_floor)) * p2
        modulus = modulus_floor + (1.0 - modulus_floor) * p3
        refs[6][352 + z : 353 + z] = modulus[0:1]
        refs[7][352 + z : 353 + z] = modulus[15:16]
        zero = jnp.zeros_like(direct)
        a = jnp.where(inside, direct * gain, zero)
        b = jnp.where(inside, p15 * gain, zero)
        a_ref[z] = a
        b_ref[z] = b
        e_ref[z] = direct * kept
        f_ref[z] = p15 * kept
        up_ref, down_ref = refs[4 + 2 * ph : 6 + 2 * ph]
        for number, value in ((0, a), (1, b)):
            start = number * 176
            if 1 <= j <= 8:
                start += (j - 1) * 8
                up_ref[start : start + 8] = value[0:8]
                down_ref[start : start + 8] = value[8:16]
            elif j >= 9:
                start += 64 + (j - 9) * 16
                up_ref[start : start + 16] = value
                down_ref[start : start + 16] = value


def force_part(p0_ref, p1_ref, fields_ref, upper_ref, lower_ref, mat_ref, out_ref, field, halo, rim):
    halo[...] = jnp.zeros(halo.shape, f32)
    rim[pl.ds(2, 32, stride=2)] = upper_ref[352:384]
    rim[pl.ds(3, 32, stride=2)] = lower_ref[352:384]
    for c in range(3):
        field[c, 0] = jnp.zeros((16, 128), f32)
        field[c, 33] = jnp.zeros((16, 128), f32)
        for k in range(16):
            start = 192 + c * 4
            halo[c, 4 * k + 2 : 4 * k + 6] = fields_ref[k, start : start + 4] * rim[4 * k + 2 : 4 * k + 6]
    for z in range(32):
        printed = (p0_ref, p1_ref)[z // 16][z % 16]
        modulus = modulus_floor + (1.0 - modulus_floor) * (printed * printed * printed)
        for c in range(3):
            field[c, z + 1] = modulus * layer_of(fields_ref, c, z)

    def body(i, carry):
        pick = product(field, halo, mat_ref, 1, i)
        low = lane((16, 128)) < 64
        for pair in range(2):
            for c in range(3):
                first = pltpu.roll(pick(pair, c, 0), 96, 1)
                second = pltpu.roll(pick(pair, c, 1), 32, 1)
                out_ref[2 * i + pair, c] = jnp.where(low, first, second)
        return carry

    lax.fori_loop(0, 8, body, 0)


def backward(ph, a_ref, b_ref, e_ref, f_ref, upper_ref, lower_ref, *refs):
    keep_up, keep_down = edges_of()
    if ph == 1:
        sens_ref, state_ref = refs
        current = None
    else:
        own_ref, su_ref, sd_ref, sens1_ref, force_ref, out_ref = refs
        current = jnp.concatenate([su_ref[...] * keep_up, own_ref[...], sd_ref[...] * keep_down], 0)
    rows = 48
    low = lane((16, 128)) < 64
    later = None
    for j in range(15, -1, -1):
        z = 16 * ph + j
        count = 48 if j >= 9 else (32 if j >= 1 else 16)
        sens = e_ref[z]
        coef = []
        for number, ref in ((0, a_ref), (1, b_ref)):
            value = ref[z]
            if j >= 1:
                size = 8 if j <= 8 else 16
                start = number * 176 + ((j - 1) * 8 if j <= 8 else 64 + (j - 9) * 16)
                value = jnp.concatenate(
                    [
                        upper_ref[start : start + size] * keep_up,
                        value,
                        lower_ref[start : start + size] * keep_down,
                    ],
                    0,
                )
            coef.append(value)
        if current is None:
            current = coef[0]
        else:
            cross = cross_of(current)
            edge = (rows - 16) // 2
            sens = sens + f_ref[z] * cross[edge : edge + 16]
            if count < rows:
                cross = cross[8 : rows - 8]
            current = coef[0] + coef[1] * cross
        rows = count
        if j % 2 == 1:
            later = pltpu.roll(sens, 32, 1)
        else:
            packed = jnp.where(low, pltpu.roll(sens, 96, 1), later)
            if ph == 1:
                sens_ref[j // 2] = packed
            else:
                out_ref[j // 2, 3] = packed
    if ph == 1:
        state_ref[...] = current
    else:
        out_ref[:, 0:3] = force_ref[...]
        for i in range(8):
            out_ref[8 + i, 3] = sens1_ref[i]


def unpack(in_ref, force_ref, sens_ref):
    low = lane((16, 128)) < 64
    for k in range(8):
        for c in range(4):
            first, second = in_ref[2 * k, c], in_ref[2 * k + 1, c]
            layers = (
                jnp.where(low, first, pltpu.roll(second, 64, 1)),
                jnp.where(low, pltpu.roll(first, 64, 1), second),
            )
            for i in range(2):
                if c < 3:
                    force_ref[c, i, :, 128 * k : 128 * k + 128] = layers[i]
                else:
                    sens_ref[i, :, 128 * k : 128 * k + 128] = layers[i]


def trade(to_lower, to_upper):
    count = lax.axis_size("lat")
    up = [(i, (i + 1) % count) for i in range(count)]
    down = [(j, i) for i, j in up]
    return lax.ppermute(to_lower, "lat", up), lax.ppermute(to_upper, "lat", down)


def exchange(x):
    return lax.all_to_all(x, "build", 0, 0, tiled=True)


def on_device(density, support_mask, pattern, blocks, displacement, adjoint):
    (windows,) = call(prepare_density, [((16, 2, 16, 256), f32)], [density])
    dens = exchange(windows).reshape(32, 16, 256)
    up, down = call(pack_edges, [((16, 1024), f32)] * 2, [displacement, adjoint])
    upper, lower = trade(down, up)
    fields, base = call(
        prepare_fields,
        [((16, 216, 128), f32), ((16, 256), f32)],
        [displacement, adjoint, support_mask, upper, lower],
        scratch=[pltpu.VMEM((16, 11 * 128), f32)],
    )
    fields = exchange(fields)
    up0, down0, up1, down1 = call(
        pack_density, [((192, 256), f32)] * 2 + [((176, 256), f32)] * 2, [dens, base], micros=0.2
    )
    upper0, lower0 = trade(down0, up0)
    upper1, lower1 = trade(down1, up1)
    layer = ((16, 16, 128), f32)
    p0, g0, k0, state = call(
        functools.partial(forward, 0),
        [layer] * 3 + [((16, 256), f32)],
        [dens, upper0, lower0, base],
        micros=2.0,
    )
    state_up, state_down = trade(state, state)
    (mats,) = call(matrices, [((4, 288, 256), bf16)], [pattern, blocks], smem=2, micros=1.4)
    p1, g1, k1, _ = call(
        functools.partial(forward, 1),
        [layer] * 3 + [((16, 256), f32)],
        [dens, upper1, lower1, state, state_up, state_down],
        micros=2.0,
    )
    work = [pltpu.VMEM((3, 34, 16, 128), f32), pltpu.VMEM((3, 72, 128), f32)]
    whole = ((32, 16, 128), f32)
    (d0,) = call(direct_part, [whole], [fields, mats], scratch=work, micros=3.0)
    rim = ((352, 128), f32)
    rim_rows = ((384, 128), f32)
    a, b, e, f, up0, down0, up1, down1 = call(
        coefficients,
        [whole] * 4 + [rim] * 2 + [rim_rows] * 2,
        [p0, g0, k0, p1, g1, k1, d0],
        micros=0.3,
    )
    upper1, lower1 = trade(down1, up1)
    upper0, lower0 = trade(down0, up0)
    (force,) = call(
        force_part,
        [((16, 3, 16, 128), f32)],
        [p0, p1, fields, upper1, lower1, mats],
        scratch=work + [pltpu.VMEM((72, 128), f32)],
        micros=3.0,
    )
    sens1, state = call(
        functools.partial(backward, 1),
        [((8, 16, 128), f32), ((16, 128), f32)],
        [a, b, e, f, upper1, lower1],
    )
    state_up, state_down = trade(state, state)
    (packed,) = call(
        functools.partial(backward, 0),
        [((16, 4, 16, 128), f32)],
        [a, b, e, f, upper0, lower0, state, state_up, state_down, sens1, force],
    )
    packed = exchange(packed)
    return tuple(call(unpack, [((3, 2, 16, 1024), f32), ((2, 16, 1024), f32)], [packed]))


def solution(mesh):
    in_specs = (
        P("build", "lat", None),
        P("lat", None),
        P(),
        P(),
        P(None, "build", "lat", None),
        P(None, "build", "lat", None),
    )
    out_specs = (P(None, "build", "lat", None), P("build", "lat", None))
    return jax.shard_map(
        on_device, mesh=mesh, in_specs=in_specs, out_specs=out_specs, check_vma=False
    )
```

```python
import functools

import jax
import jax.numpy as jnp
from jax import lax
from jax.experimental import pallas as pl
from jax.experimental.pallas import tpu as pltpu
from jax.sharding import PartitionSpec as P


smooth_eps = 0.0001
root_eps = 0.01
base_floor = 0.05
modulus_floor = 0.001
f32 = jnp.float32
bf16 = jnp.bfloat16
VM = pl.BlockSpec(memory_space=pltpu.VMEM)
SM = pl.BlockSpec(memory_space=pltpu.SMEM)


def call(kernel, outs, args, scratch=(), smem=0, micros=1.0, room=6):
    specs = [SM] * smem + [VM] * (len(args) - smem)
    name = getattr(kernel, "func", kernel).__name__
    if isinstance(kernel, functools.partial):
        name += str(kernel.args[0])
    return run(kernel, outs, args, specs, scratch, micros, room)


def run(kernel, outs, args, specs, scratch, micros, room):
    return pl.pallas_call(
        kernel,
        out_shape=[jax.ShapeDtypeStruct(s, d) for s, d in outs],
        in_specs=specs,
        out_specs=[VM] * len(outs),
        scratch_shapes=list(scratch),
        compiler_params=pltpu.CompilerParams(vmem_limit_bytes=room << 20),
        cost_estimate=pl.CostEstimate(
            flops=0, bytes_accessed=int(micros * 3690000), transcendentals=0
        ),
    )(*args)


def lane(shape):
    return lax.broadcasted_iota(jnp.int32, shape, len(shape) - 1)


def row(shape):
    return lax.broadcasted_iota(jnp.int32, shape, len(shape) - 2)


def shifted_tiles(x):
    tiles = x.shape[1] // 128
    moved = pltpu.roll(x, 32, 1)
    cut = [moved[:, 128 * t : 128 * t + 128] for t in range(tiles)]
    low = lane(cut[0].shape) < 32
    zero = jnp.zeros_like(cut[0])
    return (
        [zero, jnp.where(low, zero, cut[0])]
        + cut[1:]
        + [jnp.where(low, cut[0], zero), zero]
    )


def prepare_density(dens_ref, out_ref):
    x = dens_ref[...].reshape(32, 1024)
    s = shifted_tiles(x)
    w = [pltpu.roll(t, 64, 1) for t in s]
    low = lane(s[0].shape) < 64
    for p in range(16):
        k = p // 2 + 1
        if p % 2 == 0:
            first, second = s[k], jnp.where(low, s[k + 1], s[k - 1])
        else:
            first, second = jnp.where(low, w[k], w[k + 1]), jnp.where(low, w[k + 1], w[k])
        out_ref[p, 0:2] = first.reshape(2, 16, 128)
        shared = (lane((16, 128)) >= 32) & (lane((16, 128)) < 96)
        out_ref[p, 2] = jnp.where(shared, pltpu.roll(second[16:32], 64, 1), second[0:16])


def pack_edges(disp_ref, adj_ref, up_ref, down_ref):
    for number, ref in ((0, disp_ref), (3, adj_ref)):
        for c in range(3):
            for i in range(2):
                start = (number + c) * 2 + i
                up_ref[start : start + 1] = ref[c, i, 0:1]
                down_ref[start : start + 1] = ref[c, i, 15:16]


def prepare_fields(disp_ref, adj_ref, mask_ref, upper_ref, lower_ref, out_ref, base_ref, wide_ref):
    def tiles_of(x):
        s = shifted_tiles(x)
        w = [pltpu.roll(t, 64, 1) for t in s]
        low = lane(s[0].shape) < 64
        for p in range(16):
            k = p // 2 + 1
            yield p, s[k] if p % 2 == 0 else jnp.where(low, w[k], w[k + 1])

    for number, ref in ((0, disp_ref), (3, adj_ref)):
        for c in range(3):
            start = (number + c) * 32
            for p, tile in tiles_of(ref[c].reshape(32, 1024)):
                out_ref[p, start : start + 32] = tile
    for h, (ref, keep) in enumerate(zip((upper_ref, lower_ref), edges_of())):
        for p, tile in tiles_of(ref[...] * keep):
            out_ref[p, pl.ds(192 + h, 12, stride=2)] = tile[0:12]
    base = base_floor + (1.0 - base_floor) * mask_ref[...].astype(f32)
    for t, tile in enumerate(shifted_tiles(base)):
        wide_ref[:, 128 * t : 128 * t + 128] = tile
    p = lax.axis_index("build")
    k = lax.div(p, 2)
    odd = (p - 2 * k).astype(f32)
    before, here, after = [wide_ref[:, pl.ds(pl.multiple_of((k + t) * 128, 128), 128)] for t in range(3)]
    here2, after2 = pltpu.roll(here, 64, 1), pltpu.roll(after, 64, 1)
    low = lane(here.shape) < 64
    even0, even1 = here, jnp.where(low, after, before)
    odd0, odd1 = jnp.where(low, here2, after2), jnp.where(low, after2, here2)
    base_ref[:, 0:128] = even0 * (1.0 - odd) + odd0 * odd
    base_ref[:, 128:256] = even1 * (1.0 - odd) + odd1 * odd


def matrices(pattern_ref, blocks_ref, out_ref):
    k = lane((8, 256))
    dk = jnp.where(k < 192, k >> 6, (k - 192) >> 3)
    zk = jnp.where(k < 192, (k >> 4) & 3, ((k - 192) >> 1) & 3)
    at = [[(dk == d) & (zk == z) for z in range(4)] for d in range(3)]
    k2 = lane((16, 256))
    xk = jnp.where(k2 < 192, k2 & 15, jnp.where((k2 & 1) == 0, -1, 16))
    step = xk - row((16, 256))
    for kind in range(2):
        for ds in (-1, 0, 1):
            for c in range(3):
                rows = [[None] * 3, [None] * 3]
                for db in (-1, 0, 1):
                    values = {}
                    for da in (-1, 0, 1):
                        sign = -1 if kind == 0 else 1
                        o = 9 * (sign * da + 1) + 3 * (sign * db + 1) + (sign * ds + 1)
                        start = pattern_ref[o]
                        for d in range(3):
                            values[da, d] = (
                                blocks_ref[start, d, c] if kind == 0 else blocks_ref[start, c, d]
                            )
                    for zi in range(2):
                        r = jnp.zeros((8, 256), f32)
                        for da in (-1, 0, 1):
                            for d in range(3):
                                r = jnp.where(at[d][da + 1 + zi], values[da, d], r)
                        rows[zi][db + 1] = r
                for zi in range(2):
                    m = jnp.zeros((16, 256), f32)
                    for db in (-1, 0, 1):
                        r = rows[zi][db + 1]
                        m = jnp.where(step == db, jnp.concatenate([r, r], 0), m)
                    high = m.astype(bf16)
                    low = (m - high.astype(f32)).astype(bf16)
                    start = ((ds + 1) * 6 + c * 2 + zi) * 16
                    out_ref[2 * kind, start : start + 16] = high
                    out_ref[2 * kind + 1, start : start + 16] = low


def rim_start(j):
    return 32 + 15 * j - j * (j - 1) // 2


def shared_start(m):
    return 160 + 16 * m - m * m


def pack_rims(ph, dens_ref, state, up_ref, down_ref):
    for ref in (up_ref, down_ref):
        ref[152:160] = jnp.zeros((8, 128), f32)
        ref[224:232] = jnp.zeros((8, 128), f32)
        ref[0:16] = state[:, 0:128]
        ref[16:32] = state[:, 128:256]
    for j in range(15):
        k = 8 * ph + j // 2
        for x, start, count in (
            (dens_ref[k, j % 2], rim_start(j), 15 - j),
            (dens_ref[k, 2], shared_start(j // 2), 15 - j),
        )[: 2 - j % 2]:
            up_ref[start : start + count] = x[0:count]
            down_ref[start : start + count] = x[16 - count : 16]


def pack_density(dens_ref, base_ref, up_ref, down_ref):
    pack_rims(0, dens_ref, base_ref[...], up_ref, down_ref)


def cross_of(x):
    rows, width = x.shape
    return (
        x
        + pltpu.roll(x, 1, 0)
        + pltpu.roll(x, rows - 1, 0)
        + pltpu.roll(x, 1, 1)
        + pltpu.roll(x, width - 1, 1)
    )


def forward(ph, dens_ref, upper_ref, lower_ref, own_ref, *refs):
    up, down = [jnp.concatenate([ref[0:16], ref[16:32]], 1) for ref in (upper_ref, lower_ref)]
    printed_ref, gain_ref, kept_ref = refs[:3]
    p, q = lax.axis_index("build"), lax.axis_index("lat")
    current = jnp.concatenate([up, own_ref[...], down], 0)
    l = lane((48, 256))
    y = 64 * p - 32 + l - jnp.where(l < 192, 0, 256)
    x = 16 * q - 16 + row((48, 256))
    inside = jnp.where((x >= 0) & (x < 256) & (y >= 0) & (y < 1024), 1.0, 0.0)
    rows = 48
    for j in range(16):
        p2 = current * current
        p4 = p2 * p2
        p8 = p4 * p4
        edge = (48 - rows) // 2
        cross = cross_of(p8 * p8 * inside[edge : 48 - edge])
        count = 48 if j < 7 else (32 if j < 15 else 16)
        if count < rows:
            cross = cross[8 : rows - 8]
        rows = count
        k = 8 * ph + j // 2
        first, second = dens_ref[k, j % 2], dens_ref[k, 2]
        if j < 15:
            size = 16 if j < 7 else 8
            start, start2 = rim_start(j), shared_start(j // 2)
            end, end2 = start + 15 - j, start2 + 15 - j // 2 * 2
            first = jnp.concatenate(
                [upper_ref[end - size : end], first, lower_ref[start : start + size]], 0
            )
            second = jnp.concatenate(
                [upper_ref[end2 - size : end2], second, lower_ref[start2 : start2 + size]], 0
            )
        if j % 2 == 1:
            second = pltpu.roll(second, 64, 1)
        design = jnp.concatenate([first, second], 1)
        support = lax.rsqrt(lax.rsqrt(lax.rsqrt(lax.rsqrt(cross))))
        differ = design - support
        square = differ * differ + smooth_eps
        inverse = lax.rsqrt(square)
        current = 0.5 * (design + support - square * inverse + root_eps)
        edge = (rows - 16) // 2
        printed_ref[j] = current[edge : edge + 16, 0:128]
        slope = (differ * inverse)[edge : edge + 16, 0:128]
        s1 = support[edge : edge + 16, 0:128]
        s3 = s1 * s1 * s1
        s6 = s3 * s3
        gain_ref[j] = 0.5 * (1.0 + slope) / (s6 * s6 * s3)
        kept_ref[j] = 0.5 * (1.0 - slope)
    if ph == 0:
        state_ref, up_ref, down_ref = refs[3:]
        state_ref[...] = current
        pack_rims(1, dens_ref, current, up_ref, down_ref)


def layer_of(fields_ref, c, z):
    start = (c * 2 + z % 2) * 16
    return fields_ref[z // 2, start : start + 16]


def product(field, halo, mat_ref, kind, i):
    edges = [halo[d, pl.ds(pl.multiple_of(8 * i, 8), 16)] for d in range(3)]
    sides = []
    for pair in range(2):
        main = [field[d, pl.ds(4 * i + 2 * pair, 4)].reshape(64, 128) for d in range(3)]
        rim = [e[4 * pair : 4 * pair + 8] for e in edges]
        sides.append(jnp.concatenate(main + rim + [jnp.zeros((40, 128), f32)], 0))
    u = jnp.concatenate(sides, 1)
    high = u.astype(bf16)
    low = (u - high.astype(f32)).astype(bf16)
    dot = functools.partial(jnp.dot, preferred_element_type=f32)
    both = dot(mat_ref[2 * kind : 2 * kind + 2].reshape(576, 256), high)
    out = both[0:288] + both[288:576] + dot(mat_ref[2 * kind], low)

    def pick(pair, c, zi):
        parts = [
            out[(s * 6 + c * 2 + zi) * 16 : (s * 6 + c * 2 + zi) * 16 + 16, 128 * pair : 128 * pair + 128]
            for s in range(3)
        ]
        return parts[1] + pltpu.roll(parts[0], 1, 1) + pltpu.roll(parts[2], 127, 1)

    return pick


def edges_of():
    q = lax.axis_index("lat")
    return jnp.where(q > 0, 1.0, 0.0), jnp.where(q < 15, 1.0, 0.0)


def direct_part(fields_ref, mat_ref, out_ref, field, halo):
    halo[...] = jnp.zeros(halo.shape, f32)
    for c in range(3):
        field[c, 0] = jnp.zeros((16, 128), f32)
        field[c, 33] = jnp.zeros((16, 128), f32)
        for z in range(32):
            field[c, z + 1] = layer_of(fields_ref, 3 + c, z)
        for k in range(16):
            start = 192 + (3 + c) * 4
            halo[c, 4 * k + 2 : 4 * k + 6] = fields_ref[k, start : start + 4]

    def body(i, carry):
        pick = product(field, halo, mat_ref, 0, i)
        for pair in range(2):
            for zi in range(2):
                total = fields_ref[2 * i + pair, zi * 16 : zi * 16 + 16] * pick(pair, 0, zi)
                for c in (1, 2):
                    start = (c * 2 + zi) * 16
                    total = total + fields_ref[2 * i + pair, start : start + 16] * pick(pair, c, zi)
                out_ref[4 * i + 2 * pair + zi] = total
        return carry

    lax.fori_loop(0, 8, body, 0)


def coef_start(number, ph, j):
    return 32 + (number * 2 + ph) * 120 + j * (j - 1) // 2


def coefficients(p0_ref, g0_ref, k0_ref, p1_ref, g1_ref, k1_ref, d0_ref, *refs):
    a_ref, b_ref, e_ref, f_ref = refs[:4]
    y = 64 * lax.axis_index("build") - 32 + lane((16, 128))
    inside = (y >= 0) & (y < 1024)
    for z in range(32):
        ph, j = divmod(z, 16)
        printed = (p0_ref, p1_ref)[ph][j]
        gain = (g0_ref, g1_ref)[ph][j]
        kept = (k0_ref, k1_ref)[ph][j]
        p2 = printed * printed
        p3 = p2 * printed
        p6 = p3 * p3
        p15 = p6 * p6 * p3
        direct = d0_ref[z] * (3.0 * (1.0 - modulus_floor)) * p2
        modulus = modulus_floor + (1.0 - modulus_floor) * p3
        refs[4][z : z + 1] = modulus[0:1]
        refs[5][z : z + 1] = modulus[15:16]
        zero = jnp.zeros_like(direct)
        a = jnp.where(inside, direct * gain, zero)
        b = jnp.where(inside, p15 * gain, zero)
        a_ref[z] = a
        b_ref[z] = b
        e_ref[z] = direct * kept
        f_ref[z] = p15 * kept
        up_ref, down_ref = refs[4:6]
        for number, value in ((0, a), (1, b)):
            start = coef_start(number, ph, j)
            if j >= 1:
                up_ref[start : start + j] = value[0:j]
                down_ref[start : start + j] = value[16 - j : 16]
    for ref in refs[4:6]:
        ref[512:520] = jnp.zeros((8, 128), f32)


def force_part(p0_ref, p1_ref, fields_ref, upper_ref, lower_ref, mat_ref, out_ref, field, halo, rim):
    halo[...] = jnp.zeros(halo.shape, f32)
    rim[pl.ds(2, 32, stride=2)] = upper_ref[0:32]
    rim[pl.ds(3, 32, stride=2)] = lower_ref[0:32]
    for c in range(3):
        field[c, 0] = jnp.zeros((16, 128), f32)
        field[c, 33] = jnp.zeros((16, 128), f32)
        for k in range(16):
            start = 192 + c * 4
            halo[c, 4 * k + 2 : 4 * k + 6] = fields_ref[k, start : start + 4] * rim[4 * k + 2 : 4 * k + 6]
    for z in range(32):
        printed = (p0_ref, p1_ref)[z // 16][z % 16]
        modulus = modulus_floor + (1.0 - modulus_floor) * (printed * printed * printed)
        for c in range(3):
            field[c, z + 1] = modulus * layer_of(fields_ref, c, z)

    def body(i, carry):
        pick = product(field, halo, mat_ref, 1, i)
        low = lane((16, 128)) < 64
        for pair in range(2):
            for c in range(3):
                first = pltpu.roll(pick(pair, c, 0), 96, 1)
                second = pltpu.roll(pick(pair, c, 1), 32, 1)
                out_ref[2 * i + pair, c] = jnp.where(low, first, second)
        return carry

    lax.fori_loop(0, 8, body, 0)


def backward(ph, a_ref, b_ref, e_ref, f_ref, upper_ref, lower_ref, *refs):
    keep_up, keep_down = edges_of()
    if ph == 1:
        sens_ref, state_ref = refs
        current = None
    else:
        own_ref, su_ref, sd_ref, sens1_ref, force_ref, out_ref = refs
        current = jnp.concatenate([su_ref[...] * keep_up, own_ref[...], sd_ref[...] * keep_down], 0)
    rows = 48
    low = lane((16, 128)) < 64
    later = None
    for j in range(15, -1, -1):
        z = 16 * ph + j
        count = 48 if j >= 9 else (32 if j >= 1 else 16)
        sens = e_ref[z]
        coef = []
        for number, ref in ((0, a_ref), (1, b_ref)):
            value = ref[z]
            if j >= 1:
                size = 8 if j <= 8 else 16
                start = coef_start(number, ph, j)
                end = start + j
                value = jnp.concatenate(
                    [
                        upper_ref[end - size : end] * keep_up,
                        value,
                        lower_ref[start : start + size] * keep_down,
                    ],
                    0,
                )
            coef.append(value)
        if current is None:
            current = coef[0]
        else:
            cross = cross_of(current)
            edge = (rows - 16) // 2
            sens = sens + f_ref[z] * cross[edge : edge + 16]
            if count < rows:
                cross = cross[8 : rows - 8]
            current = coef[0] + coef[1] * cross
        rows = count
        if j % 2 == 1:
            later = pltpu.roll(sens, 32, 1)
        else:
            packed = jnp.where(low, pltpu.roll(sens, 96, 1), later)
            if ph == 1:
                sens_ref[j // 2] = packed
            else:
                out_ref[j // 2, 3] = packed
    if ph == 1:
        state_ref[...] = current
    else:
        out_ref[:, 0:3] = force_ref[...]
        for i in range(8):
            out_ref[8 + i, 3] = sens1_ref[i]


def unpack(in_ref, force_ref, sens_ref):
    low = lane((16, 128)) < 64
    for k in range(8):
        for c in range(4):
            first, second = in_ref[2 * k, c], in_ref[2 * k + 1, c]
            layers = (
                jnp.where(low, first, pltpu.roll(second, 64, 1)),
                jnp.where(low, pltpu.roll(first, 64, 1), second),
            )
            for i in range(2):
                if c < 3:
                    force_ref[c, i, :, 128 * k : 128 * k + 128] = layers[i]
                else:
                    sens_ref[i, :, 128 * k : 128 * k + 128] = layers[i]


def trade(to_lower, to_upper):
    count = lax.axis_size("lat")
    up = [(i, (i + 1) % count) for i in range(count)]
    down = [(j, i) for i, j in up]
    return lax.ppermute(to_lower, "lat", up), lax.ppermute(to_upper, "lat", down)


def exchange(x):
    return lax.all_to_all(x, "build", 0, 0, tiled=True)


def on_device(density, support_mask, pattern, blocks, displacement, adjoint):
    (windows,) = call(prepare_density, [((16, 3, 16, 128), f32)], [density])
    dens = exchange(windows)
    up, down = call(pack_edges, [((16, 1024), f32)] * 2, [displacement, adjoint])
    upper, lower = trade(down, up)
    fields, base = call(
        prepare_fields,
        [((16, 216, 128), f32), ((16, 256), f32)],
        [displacement, adjoint, support_mask, upper, lower],
        scratch=[pltpu.VMEM((16, 11 * 128), f32)],
    )
    fields = exchange(fields)
    sides = [((232, 128), f32)] * 2
    up, down = call(pack_density, sides, [dens, base], micros=0.2)
    upper, lower = trade(down, up)
    layer = ((16, 16, 128), f32)
    p0, g0, k0, state, up, down = call(
        functools.partial(forward, 0),
        [layer] * 3 + [((16, 256), f32)] + sides,
        [dens, upper, lower, base],
        micros=2.0,
    )
    upper, lower = trade(down, up)
    (mats,) = call(matrices, [((4, 288, 256), bf16)], [pattern, blocks], smem=2, micros=1.4)
    p1, g1, k1 = call(
        functools.partial(forward, 1), [layer] * 3, [dens, upper, lower, state], micros=2.0
    )
    work = [pltpu.VMEM((3, 34, 16, 128), f32), pltpu.VMEM((3, 72, 128), f32)]
    whole = ((32, 16, 128), f32)
    (d0,) = call(direct_part, [whole], [fields, mats], scratch=work, micros=3.0)
    a, b, e, f, up, down = call(
        coefficients,
        [whole] * 4 + [((520, 128), f32)] * 2,
        [p0, g0, k0, p1, g1, k1, d0],
        micros=0.3,
    )
    upper, lower = trade(down, up)
    (force,) = call(
        force_part,
        [((16, 3, 16, 128), f32)],
        [p0, p1, fields, upper, lower, mats],
        scratch=work + [pltpu.VMEM((72, 128), f32)],
        micros=3.0,
    )
    sens1, state = call(
        functools.partial(backward, 1),
        [((8, 16, 128), f32), ((16, 128), f32)],
        [a, b, e, f, upper, lower],
    )
    state_up, state_down = trade(state, state)
    (packed,) = call(
        functools.partial(backward, 0),
        [((16, 4, 16, 128), f32)],
        [a, b, e, f, upper, lower, state, state_up, state_down, sens1, force],
    )
    packed = exchange(packed)
    return tuple(call(unpack, [((3, 2, 16, 1024), f32), ((2, 16, 1024), f32)], [packed]))


def solution(mesh):
    in_specs = (
        P("build", "lat", None),
        P("lat", None),
        P(),
        P(),
        P(None, "build", "lat", None),
        P(None, "build", "lat", None),
    )
    out_specs = (P(None, "build", "lat", None), P("build", "lat", None))
    return jax.shard_map(
        on_device, mesh=mesh, in_specs=in_specs, out_specs=out_specs, check_vma=False
    )
```
